32 devices in a mesh: group: 2 (over x), dp: 16 (over z, y, core).
Axes of the slice: x: 2, y: 2, z: 4, core: 2. Of those that a mesh axis runs over, the one named last changes fastest.
Arguments:
- candidate_queries: bfloat16 [256, 8, 16, 4096], P(('group', 'dp')), parts along dimension 0, may hold values from -10 to 10
- target_states: bfloat16 [256, 32, 1024], P(('group', 'dp')), parts along dimension 0, may hold values from -4 to 4
- target_queries: bfloat16 [256, 32, 4096], P(('group', 'dp')), parts along dimension 0, may hold values from -10 to 10
- candidate_states: bfloat16 [2048, 16, 1024], P(('group', 'dp')), parts along dimension 0, may hold values from -4 to 4
- target_length: int32 [256], P(('group', 'dp')), parts along dimension 0, may hold values from 2 to 32
- candidate_length: int32 [256, 8], P(('group', 'dp')), parts along dimension 0, may hold values from 2 to 16
- candidate_row: int32 [256, 8], P(('group', 'dp')), parts along dimension 0, may hold values from 0 to 63, as said below
- direct_readout: bfloat16 [4096], replicated, may hold values from -0.5 to 0.5
- channel_readout: bfloat16 [4096], replicated, may hold values from -0.5 to 0.5
Outputs:
- rescored: float32 [2048], P(('group', 'dp')), parts along dimension 0
The draws below stay inside these ranges and needn't reach their ends.
There are 2 independent parts, one for each index of `group`. The reference program is written for one: setup_inputs(seed, part) draws one part's arguments, and reference() takes and returns one part's arrays. A program takes and returns all parts, laid end to end along the dimension named above; an argument that names none is the same for every part. Nothing has to cross between parts.
Inputs may be any that keep to these rules, and one draw needn't show every extreme that they name: `candidate_row`: on the 8 targets of each aligned block (targets b * 8 to (b + 1) * 8 - 1), the 64 entries hold every value from 0 to 63 once.
All inputs are finite; a program needn't handle non-finite values.
Results may differ from the reference program's by a relative error of at most 0.0021.
Values may be sent and summed in bfloat16 or wider, within the bound.
A program may use at most 128 MiB of HBM per device.

```python
import math
import jax
import jax.numpy as jnp
from jax import lax

TGT_DEV = 8
SLOTS = 8
TARGET_TOKENS = 32
SOURCE_TOKENS = 16
QUERY_HEADS = 32
KEY_VALUE_HEADS = 4
HEAD_SIZE = 128
QW = 4096
PART_TARGETS = 128
CAND_DEV = 64
CANDIDATE_PAIRS = 1024
PEER_ROWS = 4


def starting_values(key, shape):
    return jax.random.truncated_normal(jax.random.fold_in(key, 3), -4.0, 4.0, shape)


def draw_candidate_queries(key, part):
    value_rows = starting_values(jax.random.fold_in(key, 21), (PART_TARGETS, SLOTS, SOURCE_TOKENS, QUERY_HEADS * HEAD_SIZE))
    return value_rows.astype(jnp.bfloat16)


def draw_target_states(key, part):
    value_rows = starting_values(jax.random.fold_in(key, 22), (PART_TARGETS, TARGET_TOKENS, 2 * KEY_VALUE_HEADS * HEAD_SIZE))
    return value_rows.astype(jnp.bfloat16)


def draw_target_queries(key, part):
    value_rows = starting_values(jax.random.fold_in(key, 23), (PART_TARGETS, TARGET_TOKENS, QUERY_HEADS * HEAD_SIZE))
    return value_rows.astype(jnp.bfloat16)


def draw_candidate_states(key, part):
    value_rows = starting_values(jax.random.fold_in(key, 24), (CANDIDATE_PAIRS, SOURCE_TOKENS, 2 * KEY_VALUE_HEADS * HEAD_SIZE))
    return value_rows.astype(jnp.bfloat16)


def draw_candidate_row(key, part):
    blocks = PART_TARGETS // TGT_DEV
    block_keys = jax.random.split(jax.random.fold_in(key, 31), blocks)
    orders = jax.vmap(lambda block_key: jax.random.permutation(block_key, CAND_DEV))(block_keys)
    return orders.reshape(PART_TARGETS, SLOTS).astype(jnp.int32)


def touch_ends(array, key, smallest, high):
    longest = array.shape.index(max(array.shape))
    spots = []
    for shift in (0, 1):
        where = [jax.random.randint(jax.random.fold_in(key, axis), (), 0, length) for axis, length in enumerate(array.shape)]
        where[longest] = (where[longest] + shift) % array.shape[longest]
        spots.append(tuple(where))
    return array.at[spots[0]].set(smallest).at[spots[1]].set(high)


def bell_draw(key, extent, scale, bound, held_as=jnp.bfloat16):
    return jnp.clip(scale * jax.random.normal(key, extent, jnp.float32), -bound, bound).astype(held_as)


def setup_inputs(seed: int = 0, part: int = 0) -> dict:
    keys = jax.random.split(jax.random.key(seed), 10)
    own_keys = jax.random.split(jax.random.fold_in(keys[9], part), 10)
    return {
        "candidate_queries": draw_candidate_queries(jax.random.fold_in(jax.random.fold_in(keys[9], part), 71), part),
        "target_states": draw_target_states(jax.random.fold_in(jax.random.fold_in(keys[9], part), 71), part),
        "target_queries": draw_target_queries(jax.random.fold_in(jax.random.fold_in(keys[9], part), 71), part),
        "candidate_states": draw_candidate_states(jax.random.fold_in(jax.random.fold_in(keys[9], part), 71), part),
        "target_length": touch_ends(jax.random.randint(own_keys[4], (PART_TARGETS,), 2, TARGET_TOKENS + 1), jax.random.fold_in(own_keys[4], 1), 2, TARGET_TOKENS).astype(jnp.int32),
        "candidate_length": touch_ends(jax.random.randint(own_keys[5], (PART_TARGETS, SLOTS), 2, SOURCE_TOKENS + 1), jax.random.fold_in(own_keys[5], 1), 2, SOURCE_TOKENS).astype(jnp.int32),
        "candidate_row": draw_candidate_row(jax.random.fold_in(jax.random.fold_in(keys[9], part), 71), part),
        "direct_readout": bell_draw(keys[7], (QW,), HEAD_SIZE ** -0.5, 0.5),
        "channel_readout": bell_draw(keys[8], (QW,), HEAD_SIZE ** -0.5, 0.5),
    }


masked_score = -1e+30

def attend_one(query_rows, hidden_states, length):
    count_of_rows = query_rows.shape[0]
    length_of_keys = hidden_states.shape[0]
    grouped_heads = query_rows.reshape(count_of_rows, KEY_VALUE_HEADS, QUERY_HEADS // KEY_VALUE_HEADS, HEAD_SIZE).astype(jnp.float32)
    split_halves = hidden_states.reshape(length_of_keys, 2, KEY_VALUE_HEADS, HEAD_SIZE).astype(jnp.float32)
    scores = jnp.einsum('rgqd,kgd->gqrk', grouped_heads, split_halves[:, 0]) * (1.0 / math.sqrt(HEAD_SIZE))
    usable = jnp.arange(length_of_keys, dtype=jnp.int32) < length
    scores = jnp.where(usable, scores, masked_score)
    highest = lax.optimization_barrier(jnp.max(scores, axis=-1, keepdims=True))
    weights = jnp.exp(scores - highest)
    rounded = lax.optimization_barrier((weights / lax.optimization_barrier(jnp.sum(weights, axis=-1, keepdims=True))).astype(jnp.bfloat16))
    mixture = jnp.einsum('gqrk,kgd->rgqd', rounded.astype(jnp.float32), split_halves[:, 1])
    return mixture.astype(jnp.bfloat16).reshape(count_of_rows, QUERY_HEADS * HEAD_SIZE)

def pooled(mixture, readout, length):
    tokens = jnp.dot(mixture, readout, preferred_element_type=jnp.float32)
    usable = jnp.arange(tokens.shape[0], dtype=jnp.int32) < length
    return jnp.sum(jnp.where(usable, tokens, 0.0)) / length.astype(jnp.float32)

def reference(candidate_queries, target_states, target_queries, candidate_states, target_length, candidate_length, candidate_row, direct_readout, channel_readout):
    target_index = jnp.arange(PART_TARGETS, dtype=jnp.int32)
    stored = candidate_row // PEER_ROWS * CAND_DEV + (target_index // TGT_DEV)[:, None] * PEER_ROWS + candidate_row % PEER_ROWS

    def score_target(index):
        lengths = candidate_length[index]
        own_length = target_length[index]

        def per_slot(slot):
            direct_mix = attend_one(candidate_queries[index, slot], target_states[index], own_length)
            direct = pooled(direct_mix, direct_readout, lengths[slot])
            hidden_states = candidate_states[stored[index, slot]]
            channel_mix = attend_one(target_queries[index], hidden_states, lengths[slot])
            channel = pooled(channel_mix, channel_readout, own_length)
            return direct + channel
        return jax.vmap(per_slot)(jnp.arange(SLOTS, dtype=jnp.int32))
    combined = lax.map(score_target, target_index)
    flat_rows = stored.reshape(CANDIDATE_PAIRS)
    return jnp.zeros((CANDIDATE_PAIRS,), jnp.float32).at[flat_rows].set(combined.reshape(CANDIDATE_PAIRS))
```

```python
import functools
import math

import jax
import jax.numpy as jnp
from jax import lax
from jax.experimental import pallas as pl
from jax.experimental.pallas import tpu as pltpu
from jax.sharding import PartitionSpec as P

HEAD_SIZE = 128
AXIS = "dp"
MESH = pl.DeviceIdType.MESH
EARLY = 6
masked_score = -1e30


def dot_nt(a, b):
    return lax.dot_general(
        a, b, (((1,), (1,)), ((), ())), preferred_element_type=jnp.float32
    )


def exchange(a, b, n):
    if n & (n - 1):
        return lax.rem(a + b, n)
    out, bit = 0, 1
    while bit < n:
        out = out + lax.rem(a // bit + b // bit, 2) * bit
        bit *= 2
    return out


def expect(a, b, n):
    if n & (n - 1):
        return lax.rem(a + n - b, n)
    return exchange(a, b, n)


def ratio(scores, values, keys_left):
    keys = lax.broadcasted_iota(jnp.int32, scores.shape, 0)
    scores = jnp.where(keys < keys_left, scores, masked_score)
    highest = jnp.max(scores, axis=0, keepdims=True)
    factor = math.log2(math.e) / math.sqrt(HEAD_SIZE)
    weights = jnp.exp2((scores - highest) * factor)
    return jnp.sum(weights * values, axis=0, keepdims=True) / jnp.sum(
        weights, axis=0, keepdims=True
    )


def kernel(
    n, dims,
    table, lengths, spread, readouts, cq, ts, tq, cs,
    out,
    cq_buf, ts_buf, tq_buf, v_buf, k_buf, u_out, u_buf, ud, rd, sel, dsum, r_out, r_buf,
    in_sem, cq_sem, ks, kr, us, ur, rs, rr,
):
    T, S, I, J, H, G = dims
    C = T * S
    rpp = C // n
    hg = H // G
    D = HEAD_SIZE
    me = lax.axis_index(AXIS)

    loads = [
        pltpu.make_async_copy(cs.at[:, :, :, pl.ds(G * D, G * D)], v_buf, in_sem.at[0]),
        pltpu.make_async_copy(
            cs.at[me, :, :, pl.ds(0, G * D)], k_buf.at[me], in_sem.at[1]
        ),
        pltpu.make_async_copy(ts, ts_buf, in_sem.at[2]),
        pltpu.make_async_copy(tq, tq_buf, in_sem.at[3]),
    ]
    loads[0].start()
    loads[2].start()

    def cq_copy(t):
        return pltpu.make_async_copy(cq.at[t], cq_buf.at[t], cq_sem.at[t])

    barrier = pltpu.get_barrier_semaphore()

    def greet(k, carry):
        pl.semaphore_signal(
            barrier, inc=1, device_id={AXIS: exchange(me, k, n)}, device_id_type=MESH
        )
        return carry

    lax.fori_loop(1, n, greet, 0)
    cq_copy(0).start()

    def k_copy(p, slot):
        return pltpu.make_async_remote_copy(
            src_ref=cs.at[p, :, :, pl.ds(0, G * D)],
            dst_ref=k_buf.at[slot], send_sem=ks.at[p], recv_sem=kr.at[slot],
            device_id={AXIS: p}, device_id_type=MESH,
        )

    def u_copy(p, slot):
        return pltpu.make_async_remote_copy(
            src_ref=u_out.at[p], dst_ref=u_buf.at[slot], send_sem=us.at[p],
            recv_sem=ur.at[slot], device_id={AXIS: p}, device_id_type=MESH,
        )

    def r_copy(p, slot):
        return pltpu.make_async_remote_copy(
            src_ref=r_out.at[p], dst_ref=r_buf.at[slot], send_sem=rs.at[p],
            recv_sem=rr.at[slot], device_id={AXIS: p}, device_id_type=MESH,
        )

    def k_send(i, carry):
        p = exchange(me, n - 1 - i, n)
        k_copy(p, me).start()
        return carry

    pl.semaphore_wait(barrier, n - 1)
    early = min(EARLY, n - 1)
    lax.fori_loop(0, early, k_send, 0)
    loads[1].start()
    for t in range(1, T):
        cq_copy(t).start()
    loads[3].start()

    wide = u_out.shape[2]
    channel_r = jnp.concatenate([readouts[1]] * (wide // H), axis=0)
    row_id = lax.broadcasted_iota(jnp.int32, (wide, D), 0)
    loads[0].wait()
    u = None
    for r in range(rpp):
        for g in range(G):
            weights = jnp.where(
                row_id // hg == r * G + g, channel_r, jnp.zeros_like(channel_r)
            )
            values = v_buf[:, r, :, g * D : (g + 1) * D]
            values = values.reshape(n * I, D)
            part = dot_nt(values, weights)
            u = part if u is None else u + part
    u_out[...] = u.astype(jnp.bfloat16).reshape(n, I, wide)

    lane = lax.broadcasted_iota(jnp.int32, (wide, hg * J), 1)
    head = lax.broadcasted_iota(jnp.int32, (wide, hg * J), 0)
    for r in range(rpp):
        for g in range(G):
            hit = head == lane // J + (r * H + g * hg)
            sel[r * G + g] = jnp.where(hit, 1.0, 0.0).astype(jnp.bfloat16)

    loads[2].wait()
    rows = S * I
    for g in range(G):
        states = ts_buf[:, :, (G + g) * D : (G + g + 1) * D].reshape(T * J, D)
        for q in range(hg):
            h = g * hg + q
            rd[q * rows : (q + 1) * rows, :] = jnp.broadcast_to(
                readouts[0, h : h + 1, :], (rows, D)
            )
        ud[g] = dot_nt(states, rd[...])

    def u_send(i, carry):
        u_copy(exchange(me, n - 1 - i, n), me).start()
        return carry

    lax.fori_loop(0, n - 1, u_send, 0)
    lax.fori_loop(early, n - 1, k_send, 0)

    token = lax.rem(lax.broadcasted_iota(jnp.int32, (1, rows), 1), I)

    def direct(t, carry):
        cq_copy(t).wait()
        total = jnp.zeros((1, hg * rows), jnp.float32)
        for g in range(G):
            queries = jnp.concatenate(
                [
                    cq_buf[t, :, (g * hg + q) * D : (g * hg + q + 1) * D]
                    for q in range(hg)
                ],
                axis=0,
            )
            scores = dot_nt(ts_buf[t, :, g * D : (g + 1) * D], queries)
            values = ud[g, pl.ds(pl.multiple_of(t * J, J), J), :]
            total = total + ratio(scores, values, lengths[t])
        tokens = total[:, 0:rows]
        for q in range(1, hg):
            tokens = tokens + total[:, q * rows : (q + 1) * rows]
        count = spread[1, t]
        dsum[t] = jnp.where(token < count, tokens, 0.0) / count.astype(jnp.float32)
        return carry

    lax.fori_loop(0, T, direct, 0)

    loads[3].wait()
    lanes = out.shape[1]
    place = lax.broadcasted_iota(jnp.int32, (1, lanes), 1)
    position = lax.rem(lax.broadcasted_iota(jnp.int32, (1, hg * J), 1), J)
    direct_sums = dsum[...]
    owners = spread[0]

    def block(p):
        result = jnp.zeros((1, lanes), jnp.float32)
        sent = u_buf[p]
        for r in range(rpp):
            v = p * rpp + r
            t, source_count, target_count = table[0, v], table[1, v], table[2, v]
            total = jnp.zeros((1, hg * J), jnp.float32)
            for g in range(G):
                queries = jnp.concatenate(
                    [
                        tq_buf[t, :, (g * hg + q) * D : (g * hg + q + 1) * D]
                        for q in range(hg)
                    ],
                    axis=0,
                )
                scores = dot_nt(k_buf[p, r, :, g * D : (g + 1) * D], queries)
                values = jnp.dot(
                    sent, sel[r * G + g], preferred_element_type=jnp.float32
                )
                total = total + ratio(scores, values, source_count)
            kept = jnp.where(position < target_count, total, 0.0)
            channel = jnp.sum(kept, axis=1, keepdims=True)
            channel = channel / target_count.astype(jnp.float32)
            own = jnp.where(owners == v, direct_sums, 0.0)
            own = jnp.sum(jnp.sum(own, axis=0), axis=1, keepdims=True)
            result = result + jnp.where(place == me * rpp + r, own + channel, 0.0)
        return jnp.broadcast_to(result, (8, lanes))

    u_buf[me] = u_out[me]
    loads[1].wait()
    r_buf[me] = block(me)

    def channel_step(i, carry):
        p = expect(me, n - 1 - i, n)
        k_copy(p, p).wait_recv()
        u_copy(p, p).wait_recv()
        r_out[p] = block(p)
        r_copy(p, me).start()
        return carry

    lax.fori_loop(0, n - 1, channel_step, 0)

    def finish(i, carry):
        p = expect(me, n - 1 - i, n)
        r_copy(p, p).wait_recv()
        k_copy(p, p).wait_send()
        u_copy(p, p).wait_send()
        r_copy(p, p).wait_send()
        return carry

    lax.fori_loop(0, n - 1, finish, 0)
    out[...] = jnp.sum(r_buf[...], axis=0)


def on_device(
    n,
    candidate_queries,
    target_states,
    target_queries,
    candidate_states,
    target_length,
    candidate_length,
    candidate_row,
    direct_readout,
    channel_readout,
):
    T, S, I, QW = candidate_queries.shape
    J = target_states.shape[1]
    H = QW // HEAD_SIZE
    G = target_states.shape[2] // (2 * HEAD_SIZE)
    C = T * S
    rpp = C // n
    hg = H // G
    flat = candidate_row.reshape(C)
    each = jnp.stack(
        [
            jnp.arange(C, dtype=jnp.int32) // S,
            candidate_length.reshape(C),
            jnp.broadcast_to(target_length[:, None], (T, S)).reshape(C),
        ]
    )
    matches = flat[None, :] == jnp.arange(C, dtype=jnp.int32)[:, None]
    table = jnp.sum(jnp.where(matches[None], each[:, None, :], 0), axis=2)
    spread = jnp.broadcast_to(
        jnp.stack([candidate_row, candidate_length])[..., None], (2, T, S, I)
    ).reshape(2, T, 1, S * I)
    readouts = jnp.stack([direct_readout, channel_readout]).reshape(2, H, HEAD_SIZE)
    wide = max(128, rpp * H)
    lanes = -(-C // 128) * 128
    bf, f32 = jnp.bfloat16, jnp.float32
    vmem, smem = pltpu.VMEM, pltpu.SMEM
    anywhere = pl.BlockSpec(memory_space=pl.ANY)
    dma = pltpu.SemaphoreType.DMA
    found = pl.pallas_call(
        functools.partial(kernel, n, (T, S, I, J, H, G)),
        out_shape=jax.ShapeDtypeStruct((8, lanes), f32),
        in_specs=[
            pl.BlockSpec(memory_space=smem),
            pl.BlockSpec(memory_space=smem),
            pl.BlockSpec(memory_space=vmem),
            pl.BlockSpec(memory_space=vmem),
            anywhere, anywhere, anywhere, anywhere,
        ],
        out_specs=pl.BlockSpec(memory_space=vmem),
        scratch_shapes=[
            vmem((T, S * I, QW), bf),
            vmem(target_states.shape, bf),
            vmem(target_queries.shape, bf),
            vmem((n, rpp, I, G * HEAD_SIZE), bf),
            vmem((n, rpp, I, G * HEAD_SIZE), bf),
            vmem((n, I, wide), bf),
            vmem((n, I, wide), bf),
            vmem((G, T * J, hg * S * I), f32),
            vmem((hg * S * I, HEAD_SIZE), bf),
            vmem((rpp * G, wide, hg * J), bf),
            vmem((T, 1, S * I), f32),
            vmem((n, 8, lanes), f32),
            vmem((n, 8, lanes), f32),
            dma((4,)), dma((T,)),
            dma((n,)), dma((n,)), dma((n,)), dma((n,)), dma((n,)), dma((n,)),
        ],
        compiler_params=pltpu.CompilerParams(
            collective_id=0, has_side_effects=True, vmem_limit_bytes=60 << 20
        ),
    )(
        table, target_length, spread, readouts,
        candidate_queries.reshape(T, S * I, QW),
        target_states, target_queries,
        candidate_states.reshape(n, rpp, I, 2 * G * HEAD_SIZE),
    )
    return found[0, :C]


def solution(mesh):
    in_specs = (
        P(("group", "dp"), None, None, None),
        P(("group", "dp"), None, None),
        P(("group", "dp"), None, None),
        P(("group", "dp"), None, None),
        P(("group", "dp")),
        P(("group", "dp"), None),
        P(("group", "dp"), None),
        P(),
        P(),
    )
    return jax.shard_map(
        functools.partial(on_device, mesh.shape[AXIS]),
        mesh=mesh, in_specs=in_specs, out_specs=P(("group", "dp")), check_vma=False,
    )
```

```python
import functools
import math

import jax
import jax.numpy as jnp
from jax import lax
from jax.experimental import pallas as pl
from jax.experimental.pallas import tpu as pltpu
from jax.sharding import PartitionSpec as P

HEAD_SIZE = 128
AXIS = "dp"
MESH = pl.DeviceIdType.MESH
EARLY = 3
masked_score = -1e30


def dot_nt(a, b):
    return lax.dot_general(
        a, b, (((1,), (1,)), ((), ())), preferred_element_type=jnp.float32
    )


def exchange(a, b, n):
    if n & (n - 1):
        return lax.rem(a + b, n)
    out, bit = 0, 1
    while bit < n:
        out = out + lax.rem(a // bit + b // bit, 2) * bit
        bit *= 2
    return out


def turn(i, n):
    return lax.select(
        lax.rem(i, 2) == 0, n - 1 - i // 2, lax.max(n // 2 - 1 - i // 2, 1)
    ) if n % 2 == 0 and n > 2 else n - 1 - i


def expect(a, b, n):
    if n & (n - 1):
        return lax.rem(a + n - b, n)
    return exchange(a, b, n)


def ratio(scores, values, keys_left):
    keys = lax.broadcasted_iota(jnp.int32, scores.shape, 0)
    scores = jnp.where(keys < keys_left, scores, masked_score)
    highest = jnp.max(scores, axis=0, keepdims=True)
    factor = math.log2(math.e) / math.sqrt(HEAD_SIZE)
    weights = jnp.exp2((scores - highest) * factor)
    return jnp.sum(weights * values, axis=0, keepdims=True) / jnp.sum(
        weights, axis=0, keepdims=True
    )


def kernel(
    n, dims,
    stored, sources, lengths, direct_r, channel_r, cq, ts, tq, cs,
    out,
    cq_buf, ts_buf, tq_buf, v_buf, k_buf, u_out, u_buf, spread, ud, rd, sel, dsum, r_out, r_buf,
    in_sem, cq_sem, ks, kr, us, ur, rs, rr,
):
    T, S, I, J, H, G = dims
    C = T * S
    rpp = C // n
    hg = H // G
    D = HEAD_SIZE
    me = lax.axis_index(AXIS)

    loads = [
        pltpu.make_async_copy(cs.at[:, :, :, pl.ds(G * D, G * D)], v_buf, in_sem.at[0]),
        pltpu.make_async_copy(
            cs.at[me, :, :, pl.ds(0, G * D)], k_buf.at[me], in_sem.at[1]
        ),
        pltpu.make_async_copy(ts, ts_buf, in_sem.at[2]),
        pltpu.make_async_copy(tq, tq_buf, in_sem.at[3]),
    ]
    loads[0].start()
    loads[2].start()

    def cq_copy(t):
        return pltpu.make_async_copy(cq.at[t], cq_buf.at[t], cq_sem.at[t])

    barrier = pltpu.get_barrier_semaphore()

    def greet(k, carry):
        pl.semaphore_signal(
            barrier, inc=1, device_id={AXIS: exchange(me, k, n)}, device_id_type=MESH
        )
        return carry

    lax.fori_loop(1, n, greet, 0)
    cq_copy(0).start()

    def k_copy(p, slot):
        return pltpu.make_async_remote_copy(
            src_ref=cs.at[p, :, :, pl.ds(0, G * D)],
            dst_ref=k_buf.at[slot], send_sem=ks.at[p], recv_sem=kr.at[slot],
            device_id={AXIS: p}, device_id_type=MESH,
        )

    def u_copy(p, slot):
        return pltpu.make_async_remote_copy(
            src_ref=u_out.at[p], dst_ref=u_buf.at[slot], send_sem=us.at[p],
            recv_sem=ur.at[slot], device_id={AXIS: p}, device_id_type=MESH,
        )

    def r_copy(p, slot):
        return pltpu.make_async_remote_copy(
            src_ref=r_out.at[p], dst_ref=r_buf.at[slot], send_sem=rs.at[p],
            recv_sem=rr.at[slot], device_id={AXIS: p}, device_id_type=MESH,
        )

    def k_send(i, carry):
        p = exchange(me, turn(i, n), n)
        k_copy(p, me).start()
        return carry

    pl.semaphore_wait(barrier, n - 1)
    early = min(EARLY, n - 1)
    lax.fori_loop(0, early, k_send, 0)
    loads[1].start()
    for t in range(1, T):
        cq_copy(t).start()
    loads[3].start()

    wide = u_out.shape[2]
    head_id = lax.broadcasted_iota(jnp.int32, (H, D), 0)
    rows_r = jnp.zeros((H, D), jnp.float32)
    for h in range(H):
        row = channel_r[:, h * D : (h + 1) * D].astype(jnp.float32)
        rows_r = jnp.where(head_id == h, row, rows_r)
    rows_r = jnp.concatenate([rows_r.astype(jnp.bfloat16)] * (wide // H), axis=0)
    row_id = lax.broadcasted_iota(jnp.int32, (wide, D), 0)
    loads[0].wait()
    u = None
    for r in range(rpp):
        for g in range(G):
            weights = jnp.where(
                row_id // hg == r * G + g, rows_r, jnp.zeros_like(rows_r)
            )
            values = v_buf[:, r, :, g * D : (g + 1) * D]
            values = values.reshape(n * I, D)
            part = dot_nt(values, weights)
            u = part if u is None else u + part
    u_out[...] = u.reshape(n, I, wide)

    lane = lax.broadcasted_iota(jnp.int32, (wide, hg * J), 1)
    head = lax.broadcasted_iota(jnp.int32, (wide, hg * J), 0)
    for r in range(rpp):
        for g in range(G):
            hit = head == lane // J + (r * H + g * hg)
            sel[r * G + g] = jnp.where(hit, 1.0, 0.0).astype(jnp.bfloat16)

    def u_send(i, carry):
        u_copy(exchange(me, turn(i, n), n), me).start()
        return carry

    lax.fori_loop(0, n - 1, u_send, 0)
    lax.fori_loop(early, n - 1, k_send, 0)

    rows = S * I
    slot = lax.broadcasted_iota(jnp.int32, (1, rows), 1) // I
    for t in range(T):
        held = jnp.zeros((1, rows), jnp.int32)
        count = jnp.zeros((1, rows), jnp.int32)
        for c in range(S):
            held = jnp.where(slot == c, stored[t, c], held)
            count = jnp.where(slot == c, sources[t, c], count)
        spread[0, t] = held
        spread[1, t] = count
        spread[2, t] = (count * (J + 1) + lengths[t]) * T + t

    loads[2].wait()
    for g in range(G):
        states = ts_buf[:, :, (G + g) * D : (G + g + 1) * D].reshape(T * J, D)
        for q in range(hg):
            h = g * hg + q
            rd[q * rows : (q + 1) * rows, :] = jnp.broadcast_to(
                direct_r[:, h * D : (h + 1) * D].astype(jnp.float32), (rows, D)
            ).astype(jnp.bfloat16)
        ud[g] = dot_nt(states, rd[...])

    token = lax.rem(lax.broadcasted_iota(jnp.int32, (1, rows), 1), I)

    def direct(t, carry):
        cq_copy(t).wait()
        total = jnp.zeros((1, hg * rows), jnp.float32)
        for g in range(G):
            queries = jnp.concatenate(
                [
                    cq_buf[t, :, (g * hg + q) * D : (g * hg + q + 1) * D]
                    for q in range(hg)
                ],
                axis=0,
            )
            scores = dot_nt(ts_buf[t, :, g * D : (g + 1) * D], queries)
            values = ud[g, pl.ds(pl.multiple_of(t * J, J), J), :]
            total = total + ratio(scores, values, lengths[t])
        tokens = total[:, 0:rows]
        for q in range(1, hg):
            tokens = tokens + total[:, q * rows : (q + 1) * rows]
        count = spread[1, t]
        dsum[t] = jnp.where(token < count, tokens, 0.0) / count.astype(jnp.float32)
        return carry

    lax.fori_loop(0, T, direct, 0)

    loads[3].wait()
    lanes = out.shape[1]
    place = lax.broadcasted_iota(jnp.int32, (1, lanes), 1)
    position = lax.rem(lax.broadcasted_iota(jnp.int32, (1, hg * J), 1), J)
    direct_sums = dsum[...]
    owners = spread[0]
    codes = spread[2]

    def lookup(p):
        return [
            jnp.max(jnp.where(owners == p * rpp + r, codes, 0)) for r in range(rpp)
        ]

    def block(p, found):
        result = jnp.zeros((1, lanes), jnp.float32)
        whole = u_buf[p]
        high = whole.astype(jnp.bfloat16)
        low = (whole - high.astype(jnp.float32)).astype(jnp.bfloat16)
        sent = jnp.concatenate([high, low], axis=0)
        for r in range(rpp):
            v = p * rpp + r
            t = lax.rem(found[r], T)
            target_count = lax.rem(found[r] // T, J + 1)
            source_count = found[r] // (T * (J + 1))
            total = jnp.zeros((1, hg * J), jnp.float32)
            for g in range(G):
                queries = jnp.concatenate(
                    [
                        tq_buf[t, :, (g * hg + q) * D : (g * hg + q + 1) * D]
                        for q in range(hg)
                    ],
                    axis=0,
                )
                scores = dot_nt(k_buf[p, r, :, g * D : (g + 1) * D], queries)
                values = jnp.dot(
                    sent, sel[r * G + g], preferred_element_type=jnp.float32
                )
                values = values[:I] + values[I:]
                total = total + ratio(scores, values, source_count)
            kept = jnp.where(position < target_count, total, 0.0)
            channel = jnp.sum(kept, axis=1, keepdims=True)
            channel = channel / target_count.astype(jnp.float32)
            own = jnp.where(owners == v, direct_sums, 0.0)
            own = jnp.sum(jnp.sum(own, axis=0), axis=1, keepdims=True)
            result = result + jnp.where(place == me * rpp + r, own + channel, 0.0)
        return jnp.broadcast_to(result, (8, lanes))

    u_buf[me] = u_out[me]
    loads[1].wait()
    r_buf[me] = block(me, lookup(me))

    def channel_step(i, carry):
        p = expect(me, turn(i, n), n)
        found = lookup(p)
        k_copy(p, p).wait_recv()
        u_copy(p, p).wait_recv()
        r_out[p] = block(p, found)
        r_copy(p, me).start()
        return carry

    lax.fori_loop(0, n - 1, channel_step, 0)

    def finish(i, carry):
        p = expect(me, turn(i, n), n)
        r_copy(p, p).wait_recv()
        k_copy(p, p).wait_send()
        u_copy(p, p).wait_send()
        r_copy(p, p).wait_send()
        return carry

    lax.fori_loop(0, n - 1, finish, 0)
    out[...] = jnp.sum(r_buf[...], axis=0)


def on_device(
    n,
    candidate_queries,
    target_states,
    target_queries,
    candidate_states,
    target_length,
    candidate_length,
    candidate_row,
    direct_readout,
    channel_readout,
):
    T, S, I, QW = candidate_queries.shape
    J = target_states.shape[1]
    H = QW // HEAD_SIZE
    G = target_states.shape[2] // (2 * HEAD_SIZE)
    C = T * S
    rpp = C // n
    hg = H // G
    wide = max(128, rpp * H)
    lanes = -(-C // 128) * 128
    bf, f32 = jnp.bfloat16, jnp.float32
    vmem, smem = pltpu.VMEM, pltpu.SMEM
    anywhere = pl.BlockSpec(memory_space=pl.ANY)
    dma = pltpu.SemaphoreType.DMA
    found = pl.pallas_call(
        functools.partial(kernel, n, (T, S, I, J, H, G)),
        out_shape=jax.ShapeDtypeStruct((8, lanes), f32),
        in_specs=[
            pl.BlockSpec(memory_space=smem),
            pl.BlockSpec(memory_space=smem),
            pl.BlockSpec(memory_space=smem),
            pl.BlockSpec(memory_space=vmem),
            pl.BlockSpec(memory_space=vmem),
            anywhere, anywhere, anywhere, anywhere,
        ],
        out_specs=pl.BlockSpec(memory_space=vmem),
        scratch_shapes=[
            vmem((T, S * I, QW), bf),
            vmem(target_states.shape, bf),
            vmem(target_queries.shape, bf),
            vmem((n, rpp, I, G * HEAD_SIZE), bf),
            vmem((n, rpp, I, G * HEAD_SIZE), bf),
            vmem((n, I, wide), f32),
            vmem((n, I, wide), f32),
            vmem((3, T, 1, S * I), jnp.int32),
            vmem((G, T * J, hg * S * I), f32),
            vmem((hg * S * I, HEAD_SIZE), bf),
            vmem((rpp * G, wide, hg * J), bf),
            vmem((T, 1, S * I), f32),
            vmem((n, 8, lanes), f32),
            vmem((n, 8, lanes), f32),
            dma((4,)), dma((T,)),
            dma((n,)), dma((n,)), dma((n,)), dma((n,)), dma((n,)), dma((n,)),
        ],
        compiler_params=pltpu.CompilerParams(
            collective_id=0, has_side_effects=True, vmem_limit_bytes=60 << 20
        ),
    )(
        candidate_row, candidate_length, target_length,
        direct_readout.reshape(1, QW), channel_readout.reshape(1, QW),
        candidate_queries.reshape(T, S * I, QW),
        target_states, target_queries,
        candidate_states.reshape(n, rpp, I, 2 * G * HEAD_SIZE),
    )
    return found[0, :C]


def solution(mesh):
    in_specs = (
        P(("group", "dp"), None, None, None),
        P(("group", "dp"), None, None),
        P(("group", "dp"), None, None),
        P(("group", "dp"), None, None),
        P(("group", "dp")),
        P(("group", "dp"), None),
        P(("group", "dp"), None),
        P(),
        P(),
    )
    return jax.shard_map(
        functools.partial(on_device, mesh.shape[AXIS]),
        mesh=mesh, in_specs=in_specs, out_specs=P(("group", "dp")), check_vma=False,
    )
```

```python
import functools
import math

import jax
import jax.numpy as jnp
from jax import lax
from jax.experimental import pallas as pl
from jax.experimental.pallas import tpu as pltpu
from jax.sharding import PartitionSpec as P

HEAD_SIZE = 128
AXIS = "dp"
MESH = pl.DeviceIdType.MESH
EARLY = 3
masked_score = -1e30


def dot_nt(a, b):
    return lax.dot_general(
        a, b, (((1,), (1,)), ((), ())), preferred_element_type=jnp.float32
    )


def exchange(a, b, n):
    if n & (n - 1):
        return lax.rem(a + b, n)
    out, bit = 0, 1
    while bit < n:
        out = out + lax.rem(a // bit + b // bit, 2) * bit
        bit *= 2
    return out


def turn(i, n):
    return lax.select(
        lax.rem(i, 2) == 0, n - 1 - i // 2, lax.max(n // 2 - 1 - i // 2, 1)
    ) if n % 2 == 0 and n > 2 else n - 1 - i


def expect(a, b, n):
    if n & (n - 1):
        return lax.rem(a + n - b, n)
    return exchange(a, b, n)


def ratio(scores, values, keys_left):
    keys = lax.broadcasted_iota(jnp.int32, scores.shape, 0)
    scores = jnp.where(keys < keys_left, scores, masked_score)
    highest = jnp.max(scores, axis=0, keepdims=True)
    factor = math.log2(math.e) / math.sqrt(HEAD_SIZE)
    weights = jnp.exp2((scores - highest) * factor)
    return jnp.sum(weights * values, axis=0, keepdims=True) / jnp.sum(
        weights, axis=0, keepdims=True
    )


def kernel(
    n, dims,
    stored_in, sources_in, lengths_in, direct_in, channel_in, cq, ts, tq, cs,
    out,
    stored, sources, lengths, direct_r, channel_r,
    cq_buf, ts_buf, tq_buf, v_buf, k_buf, u_out, u_buf, spread, ud, rd, sel, dsum, r_out, r_buf,
    in_sem, cq_sem, ks, kr, us, ur, rs, rr,
):
    T, S, I, J, H, G = dims
    C = T * S
    rpp = C // n
    hg = H // G
    D = HEAD_SIZE
    me = lax.axis_index(AXIS)

    loads = [
        pltpu.make_async_copy(cs.at[:, :, :, pl.ds(G * D, G * D)], v_buf, in_sem.at[0]),
        pltpu.make_async_copy(
            cs.at[me, :, :, pl.ds(0, G * D)], k_buf.at[me], in_sem.at[1]
        ),
        pltpu.make_async_copy(ts, ts_buf, in_sem.at[2]),
        pltpu.make_async_copy(tq, tq_buf, in_sem.at[3]),
        pltpu.make_async_copy(channel_in, channel_r, in_sem.at[4]),
        pltpu.make_async_copy(direct_in, direct_r, in_sem.at[5]),
        pltpu.make_async_copy(stored_in, stored, in_sem.at[6]),
        pltpu.make_async_copy(sources_in, sources, in_sem.at[7]),
        pltpu.make_async_copy(lengths_in, lengths, in_sem.at[8]),
    ]
    def cq_copy(t):
        return pltpu.make_async_copy(cq.at[t], cq_buf.at[t], cq_sem.at[t])

    barrier = pltpu.get_barrier_semaphore()

    def greet(k, carry):
        pl.semaphore_signal(
            barrier, inc=1, device_id={AXIS: exchange(me, k, n)}, device_id_type=MESH
        )
        return carry

    lax.fori_loop(1, n, greet, 0)
    for load in loads[4:]:
        load.start()
    loads[0].start()
    loads[2].start()
    cq_copy(0).start()

    def k_copy(p, slot):
        return pltpu.make_async_remote_copy(
            src_ref=cs.at[p, :, :, pl.ds(0, G * D)],
            dst_ref=k_buf.at[slot], send_sem=ks.at[p], recv_sem=kr.at[slot],
            device_id={AXIS: p}, device_id_type=MESH,
        )

    def u_copy(p, slot):
        return pltpu.make_async_remote_copy(
            src_ref=u_out.at[p], dst_ref=u_buf.at[slot], send_sem=us.at[p],
            recv_sem=ur.at[slot], device_id={AXIS: p}, device_id_type=MESH,
        )

    def r_copy(p, slot):
        return pltpu.make_async_remote_copy(
            src_ref=r_out.at[p], dst_ref=r_buf.at[slot], send_sem=rs.at[p],
            recv_sem=rr.at[slot], device_id={AXIS: p}, device_id_type=MESH,
        )

    def k_send(i, carry):
        p = exchange(me, turn(i, n), n)
        k_copy(p, me).start()
        return carry

    pl.semaphore_wait(barrier, n - 1)
    early = min(EARLY, n - 1)
    lax.fori_loop(0, early, k_send, 0)
    loads[1].start()
    for t in range(1, T):
        cq_copy(t).start()
    loads[3].start()

    wide = u_out.shape[2]
    head_id = lax.broadcasted_iota(jnp.int32, (H, D), 0)
    rows_r = jnp.zeros((H, D), jnp.float32)
    loads[4].wait()
    for h in range(H):
        row = channel_r[h * D : (h + 1) * D].astype(jnp.float32).reshape(1, D)
        rows_r = jnp.where(head_id == h, row, rows_r)
    rows_r = jnp.concatenate([rows_r.astype(jnp.bfloat16)] * (wide // H), axis=0)
    row_id = lax.broadcasted_iota(jnp.int32, (wide, D), 0)
    loads[0].wait()
    u = None
    for r in range(rpp):
        for g in range(G):
            weights = jnp.where(
                row_id // hg == r * G + g, rows_r, jnp.zeros_like(rows_r)
            )
            values = v_buf[:, r, :, g * D : (g + 1) * D]
            values = values.reshape(n * I, D)
            part = dot_nt(values, weights)
            u = part if u is None else u + part
    u_out[...] = u.reshape(n, I, wide)

    lane = lax.broadcasted_iota(jnp.int32, (wide, hg * J), 1)
    head = lax.broadcasted_iota(jnp.int32, (wide, hg * J), 0)
    for r in range(rpp):
        for g in range(G):
            hit = head == lane // J + (r * H + g * hg)
            sel[r * G + g] = jnp.where(hit, 1.0, 0.0).astype(jnp.bfloat16)

    def u_send(i, carry):
        u_copy(exchange(me, turn(i, n), n), me).start()
        return carry

    lax.fori_loop(0, n - 1, u_send, 0)
    lax.fori_loop(early, n - 1, k_send, 0)

    rows = S * I
    slot = lax.broadcasted_iota(jnp.int32, (1, rows), 1) // I
    for load in loads[5:]:
        load.wait()
    for t in range(T):
        held = jnp.zeros((1, rows), jnp.int32)
        count = jnp.zeros((1, rows), jnp.int32)
        for c in range(S):
            held = jnp.where(slot == c, stored[t, c], held)
            count = jnp.where(slot == c, sources[t, c], count)
        spread[0, t] = held
        spread[1, t] = count
        spread[2, t] = (count * (J + 1) + lengths[t]) * T + t

    loads[2].wait()
    for g in range(G):
        states = ts_buf[:, :, (G + g) * D : (G + g + 1) * D].reshape(T * J, D)
        for q in range(hg):
            h = g * hg + q
            rd[q * rows : (q + 1) * rows, :] = jnp.broadcast_to(
                direct_r[h * D : (h + 1) * D].astype(jnp.float32).reshape(1, D), (rows, D)
            ).astype(jnp.bfloat16)
        ud[g] = dot_nt(states, rd[...])

    token = lax.rem(lax.broadcasted_iota(jnp.int32, (1, rows), 1), I)

    def direct(t, carry):
        cq_copy(t).wait()
        total = jnp.zeros((1, hg * rows), jnp.float32)
        for g in range(G):
            queries = jnp.concatenate(
                [
                    cq_buf[t, :, (g * hg + q) * D : (g * hg + q + 1) * D]
                    for q in range(hg)
                ],
                axis=0,
            )
            scores = dot_nt(ts_buf[t, :, g * D : (g + 1) * D], queries)
            values = ud[g, pl.ds(pl.multiple_of(t * J, J), J), :]
            total = total + ratio(scores, values, lengths[t])
        tokens = total[:, 0:rows]
        for q in range(1, hg):
            tokens = tokens + total[:, q * rows : (q + 1) * rows]
        count = spread[1, t]
        dsum[t] = jnp.where(token < count, tokens, 0.0) / count.astype(jnp.float32)
        return carry

    lax.fori_loop(0, T, direct, 0)

    loads[3].wait()
    lanes = out.shape[1]
    place = lax.broadcasted_iota(jnp.int32, (1, lanes), 1)
    position = lax.rem(lax.broadcasted_iota(jnp.int32, (1, hg * J), 1), J)
    direct_sums = dsum[...]
    owners = spread[0]
    codes = spread[2]

    def lookup(p):
        return [
            jnp.max(jnp.where(owners == p * rpp + r, codes, 0)) for r in range(rpp)
        ]

    def block(p, found):
        result = jnp.zeros((1, lanes), jnp.float32)
        whole = u_buf[p]
        high = whole.astype(jnp.bfloat16)
        low = (whole - high.astype(jnp.float32)).astype(jnp.bfloat16)
        sent = jnp.concatenate([high, low], axis=0)
        for r in range(rpp):
            v = p * rpp + r
            t = lax.rem(found[r], T)
            target_count = lax.rem(found[r] // T, J + 1)
            source_count = found[r] // (T * (J + 1))
            total = jnp.zeros((1, hg * J), jnp.float32)
            for g in range(G):
                queries = jnp.concatenate(
                    [
                        tq_buf[t, :, (g * hg + q) * D : (g * hg + q + 1) * D]
                        for q in range(hg)
                    ],
                    axis=0,
                )
                scores = dot_nt(k_buf[p, r, :, g * D : (g + 1) * D], queries)
                values = jnp.dot(
                    sent, sel[r * G + g], preferred_element_type=jnp.float32
                )
                values = values[:I] + values[I:]
                total = total + ratio(scores, values, source_count)
            kept = jnp.where(position < target_count, total, 0.0)
            channel = jnp.sum(kept, axis=1, keepdims=True)
            channel = channel / target_count.astype(jnp.float32)
            own = jnp.where(owners == v, direct_sums, 0.0)
            own = jnp.sum(jnp.sum(own, axis=0), axis=1, keepdims=True)
            result = result + jnp.where(place == me * rpp + r, own + channel, 0.0)
        return jnp.broadcast_to(result, (8, lanes))

    u_buf[me] = u_out[me]
    loads[1].wait()
    r_buf[me] = block(me, lookup(me))

    def channel_step(i, carry):
        p = expect(me, turn(i, n), n)
        found = lookup(p)
        k_copy(p, p).wait_recv()
        u_copy(p, p).wait_recv()
        r_out[p] = block(p, found)
        r_copy(p, me).start()
        return carry

    lax.fori_loop(0, n - 1, channel_step, 0)

    def finish(i, carry):
        p = expect(me, turn(i, n), n)
        r_copy(p, p).wait_recv()
        k_copy(p, p).wait_send()
        u_copy(p, p).wait_send()
        r_copy(p, p).wait_send()
        return carry

    lax.fori_loop(0, n - 1, finish, 0)
    out[...] = jnp.sum(r_buf[...], axis=0)


def on_device(
    n,
    candidate_queries,
    target_states,
    target_queries,
    candidate_states,
    target_length,
    candidate_length,
    candidate_row,
    direct_readout,
    channel_readout,
):
    T, S, I, QW = candidate_queries.shape
    J = target_states.shape[1]
    H = QW // HEAD_SIZE
    G = target_states.shape[2] // (2 * HEAD_SIZE)
    C = T * S
    rpp = C // n
    hg = H // G
    wide = max(128, rpp * H)
    lanes = -(-C // 128) * 128
    bf, f32 = jnp.bfloat16, jnp.float32
    vmem, smem = pltpu.VMEM, pltpu.SMEM
    anywhere = pl.BlockSpec(memory_space=pl.ANY)
    dma = pltpu.SemaphoreType.DMA
    found = pl.pallas_call(
        functools.partial(kernel, n, (T, S, I, J, H, G)),
        out_shape=jax.ShapeDtypeStruct((8, lanes), f32),
        in_specs=[
            anywhere, anywhere, anywhere, anywhere, anywhere,
            anywhere, anywhere, anywhere, anywhere,
        ],
        out_specs=pl.BlockSpec(memory_space=vmem),
        scratch_shapes=[
            smem((T, S), jnp.int32),
            smem((T, S), jnp.int32),
            smem((T,), jnp.int32),
            vmem((QW,), bf),
            vmem((QW,), bf),
            vmem((T, S * I, QW), bf),
            vmem(target_states.shape, bf),
            vmem(target_queries.shape, bf),
            vmem((n, rpp, I, G * HEAD_SIZE), bf),
            vmem((n, rpp, I, G * HEAD_SIZE), bf),
            vmem((n, I, wide), f32),
            vmem((n, I, wide), f32),
            vmem((3, T, 1, S * I), jnp.int32),
            vmem((G, T * J, hg * S * I), f32),
            vmem((hg * S * I, HEAD_SIZE), bf),
            vmem((rpp * G, wide, hg * J), bf),
            vmem((T, 1, S * I), f32),
            vmem((n, 8, lanes), f32),
            vmem((n, 8, lanes), f32),
            dma((9,)), dma((T,)),
            dma((n,)), dma((n,)), dma((n,)), dma((n,)), dma((n,)), dma((n,)),
        ],
        compiler_params=pltpu.CompilerParams(
            collective_id=0, has_side_effects=True, vmem_limit_bytes=60 << 20
        ),
    )(
        candidate_row, candidate_length, target_length,
        direct_readout, channel_readout,
        candidate_queries.reshape(T, S * I, QW),
        target_states, target_queries,
        candidate_states.reshape(n, rpp, I, 2 * G * HEAD_SIZE),
    )
    return found[0, :C]


def solution(mesh):
    in_specs = (
        P(("group", "dp"), None, None, None),
        P(("group", "dp"), None, None),
        P(("group", "dp"), None, None),
        P(("group", "dp"), None, None),
        P(("group", "dp")),
        P(("group", "dp"), None),
        P(("group", "dp"), None),
        P(),
        P(),
    )
    return jax.shard_map(
        functools.partial(on_device, mesh.shape[AXIS]),
        mesh=mesh, in_specs=in_specs, out_specs=P(("group", "dp")), check_vma=False,
    )
```
